128 devices in a mesh: dom: 64 (over z, x, y), rep: 2 (over core).
Axes of the slice: x: 4, y: 4, z: 4, core: 2. Of those that a mesh axis runs over, the one named last changes fastest.
Arguments:
- embeds: bfloat16 [65536, 1024], P(('dom', 'rep')), may hold values from -6 to 6
- weight_in: bfloat16 [1024, 4096], replicated, may hold values from -0.1875 to 0.1875
- weight_out: bfloat16 [4096, 512], replicated, may hold values from -0.09375 to 0.09375
- prototypes: bfloat16 [1000, 512], replicated, may hold values from -4 to 4
- tile_column: int32 [512, 8], P(('dom', 'rep')), may hold values from 0 to 11, as said below
- tile_weight: bfloat16 [512, 8, 128, 128], P(('dom', 'rep')), may hold values from 0 to 1
- send_rows: int32 [128, 128, 8], P(('dom', 'rep')), may hold values from 0 to 511
- send_count: int32 [128, 128], P(('dom', 'rep')), may hold values from 1 to 8, as said below
- label_rows: int32 [8192], P(('dom', 'rep')), may hold values from 0 to 511, as said below
- label_class: int32 [8192], P(('dom', 'rep')), may hold values from 0 to 999
Outputs:
- embed_grad: bfloat16 [65536, 1024], P(('dom', 'rep'))
- grad_weight_out: float32 [4096, 512], P(('dom', 'rep'))
The draws below stay inside these ranges and needn't reach their ends.
Inputs may be any that keep to these rules, and one draw needn't show every extreme that they name: `tile_column`: in each row block b the first tile names block b mod 4, tiles 1 to 3 name blocks below 4, the others name received blocks; every received block is named by some tile of its partition. `send_count`: every partition fills all 8 slots for at least one other partition. `label_rows`: distinct within a partition.
All inputs are finite; a program needn't handle non-finite values.
Results may differ from the reference program's by a relative error of at most 0.006.
The reference program's roundings to bfloat16 on the way count: a program that leaves them out, or rounds other values in their place, can miss the bound.
Values may be sent and summed in bfloat16 or wider, within the bound.
A program may use at most 128 MiB of HBM per device.

```python
import math
import jax
import jax.numpy as jnp
from jax import lax

D_IN = 1024
FF = 4096
D_OUT = 512
CLASSES = 1000
BLOCK = 128
TILES_ROW = 8
BLOCKS_DEV = 4
SEND_CAP = 8
LABELS_DEV = 64
NODE_DEV = 512
PEERS = 128
NODES = 65536
RECV_BLOCKS = 8
LABELS = 8192
N_DOM = 64
N_REP = 2


def draw_tile_column(key, part):
    half_count = TILES_ROW // 2
    key_local, key_turn = jax.random.split(key)
    shape_all = (PEERS, BLOCKS_DEV, TILES_ROW)
    local_pick = jax.random.randint(key_local, shape_all, 0, BLOCKS_DEV)
    turning = jax.random.randint(key_turn, (PEERS, 1, 1), 0, RECV_BLOCKS)
    block_index = lax.broadcasted_iota(jnp.int32, shape_all, 1)
    tile_index = lax.broadcasted_iota(jnp.int32, shape_all, 2)
    remote_order = block_index * (TILES_ROW - half_count) + (tile_index - half_count)
    remote_pick = BLOCKS_DEV + (remote_order + turning) % RECV_BLOCKS
    chosen = jnp.where(tile_index == 0, block_index, jnp.where(tile_index < half_count, local_pick, remote_pick))
    return chosen.reshape(PEERS * BLOCKS_DEV, TILES_ROW).astype(jnp.int32)


def draw_tile_weight(key, part):
    uniform_draw = jax.random.uniform(key, (PEERS * BLOCKS_DEV, TILES_ROW, BLOCK, BLOCK), jnp.float32)
    return (uniform_draw ** 96.0).astype(jnp.bfloat16)


def draw_send_count(key, part):
    counts = jax.random.randint(key, (PEERS, PEERS), 1, SEND_CAP + 1)
    sender = lax.broadcasted_iota(jnp.int32, (PEERS, PEERS), 0)
    receiver = lax.broadcasted_iota(jnp.int32, (PEERS, PEERS), 1)
    return jnp.where(receiver == (sender + 1) % PEERS, SEND_CAP, counts).astype(jnp.int32)


def pick_labels(single):
    return jax.random.permutation(single, NODE_DEV)[:LABELS_DEV]


def draw_label_rows(key, part):
    key_all = jax.random.split(key, PEERS)
    picked = jax.vmap(pick_labels)(key_all)
    return picked.reshape(PEERS * LABELS_DEV).astype(jnp.int32)


def with_ends(array, own_key, low, largest):
    longest = array.shape.index(max(array.shape))
    spots = []
    for shift in (0, 1):
        where = [jax.random.randint(jax.random.fold_in(own_key, axis), (), 0, length) for axis, length in enumerate(array.shape)]
        where[longest] = (where[longest] + shift) % array.shape[longest]
        spots.append(tuple(where))
    return array.at[spots[0]].set(low).at[spots[1]].set(largest)


def steps_of(key, extent, pieces, smallest, high):
    def one(dim, blocks):
        heights = jax.random.uniform(jax.random.fold_in(jax.random.fold_in(key, 6), dim), (blocks,), jnp.float32, smallest / len(pieces), high / len(pieces))
        return jnp.repeat(jnp.exp(heights), extent[dim] // blocks).reshape((-1,) + (1,) * (len(extent) - dim - 1))

    factor_of = one(*pieces[0])
    for cut in pieces[1:]:
        factor_of = factor_of * one(*cut)
    return factor_of


def scatter_about(key, dims, width, most, pieces=(), held_as=jnp.bfloat16):
    array = width * jax.random.normal(key, dims, jnp.float32)
    if pieces:
        array = array * steps_of(key, dims, pieces, -0.22, 0.18)
    return jnp.clip(array, -most, most).astype(held_as)


def setup_inputs(seed: int = 0) -> dict:
    arg_keys = jax.random.split(jax.random.key(seed), 11)
    embeds = scatter_about(arg_keys[0], (NODES, D_IN), 1.0, 6.0, ((0, 128),))
    weight_in = scatter_about(arg_keys[1], (D_IN, FF), D_IN ** -0.5, 0.1875)
    weight_out = scatter_about(arg_keys[2], (FF, D_OUT), FF ** -0.5, 0.09375)
    prototypes = scatter_about(arg_keys[3], (CLASSES, D_OUT), 0.5, 4.0)
    tile_column = draw_tile_column(jax.random.fold_in(arg_keys[10], 71), 0)
    tile_weight = draw_tile_weight(jax.random.fold_in(arg_keys[10], 71), 0)
    send_rows = with_ends(jax.random.randint(arg_keys[6], (PEERS, PEERS, SEND_CAP), 0, NODE_DEV), jax.random.fold_in(arg_keys[6], 1), 0, NODE_DEV - 1).astype(jnp.int32)
    send_count = draw_send_count(jax.random.fold_in(arg_keys[10], 71), 0)
    label_rows = draw_label_rows(jax.random.fold_in(arg_keys[10], 71), 0)
    label_class = with_ends(jax.random.randint(arg_keys[9], (LABELS,), 0, CLASSES), jax.random.fold_in(arg_keys[9], 1), 0, CLASSES - 1).astype(jnp.int32)
    return dict(embeds=embeds, weight_in=weight_in, weight_out=weight_out, prototypes=prototypes, tile_column=tile_column, tile_weight=tile_weight, send_rows=send_rows, send_count=send_count, label_rows=label_rows, label_class=label_class)


gelu_inner = 0.7978845608028654
gelu_cubic = 0.044715

def gelu_value(values):
    inner_arg = gelu_inner * (values + gelu_cubic * values * values * values)
    return 0.5 * values * (1.0 + jnp.tanh(inner_arg))

def gelu_slope(values):
    inner_arg = gelu_inner * (values + gelu_cubic * values * values * values)
    tangent = jnp.tanh(inner_arg)
    return 0.5 * (1.0 + tangent) + 0.5 * values * (1.0 - tangent * tangent) * gelu_inner * (1.0 + 3.0 * gelu_cubic * values * values)

def reference(embeds, weight_in, weight_out, prototypes, tile_column, tile_weight, send_rows, send_count, label_rows, label_class):
    peer_count = N_DOM * N_REP
    inputs_dev = embeds.reshape(peer_count, NODE_DEV, D_IN)

    def forward(block_in):
        pre_act = jnp.dot(block_in, weight_in, preferred_element_type=jnp.float32)
        hidden = gelu_value(pre_act).astype(jnp.bfloat16)
        return jnp.dot(hidden, weight_out, preferred_element_type=jnp.float32)
    projected = lax.map(forward, inputs_dev)
    weights_dev = tile_weight.reshape(peer_count, BLOCKS_DEV, TILES_ROW, BLOCK, BLOCK)

    def row_sums(tile_set):
        return lax.optimization_barrier(jnp.sum(tile_set.astype(jnp.float32), axis=(1, 3)))
    rowsum = lax.map(row_sums, weights_dev).reshape(peer_count, NODE_DEV)
    scaling = lax.rsqrt(1.0 + rowsum)
    unit_rows = (projected * scaling[:, :, None]).astype(jnp.bfloat16)
    slot_index = lax.broadcasted_iota(jnp.int32, (peer_count, peer_count, SEND_CAP), 2)
    slot_mask = slot_index < send_count[:, :, None]

    def pick_rows(unit_local, index_local):
        return jnp.take(unit_local, index_local, axis=0)
    picked = jax.vmap(pick_rows)(unit_rows, send_rows.reshape(peer_count, peer_count * SEND_CAP))
    picked = picked.reshape(peer_count, peer_count, SEND_CAP, D_OUT)
    picked = jnp.where(slot_mask[:, :, :, None], picked, jnp.zeros_like(picked))
    received = jnp.swapaxes(picked, 0, 1).reshape(peer_count, peer_count * SEND_CAP, D_OUT)
    columns_dev = tile_column.reshape(peer_count, BLOCKS_DEV, TILES_ROW)

    def graph_part(operands):
        unit_local, incoming, tile_set, column_set, rowsum_local = operands
        extended = jnp.concatenate([unit_local, incoming], axis=0)
        extended = extended.reshape(BLOCKS_DEV + RECV_BLOCKS, BLOCK, D_OUT).astype(jnp.float32)
        flat_columns = column_set.reshape(BLOCKS_DEV * TILES_ROW).astype(jnp.int32)
        sources = extended[flat_columns].reshape(BLOCKS_DEV, TILES_ROW, BLOCK, D_OUT)
        weight_set = tile_set.astype(jnp.float32)
        neighbour = jnp.einsum('rtab,rtbd->rad', weight_set, sources, precision=lax.Precision.HIGHEST)
        unit_float = unit_local.astype(jnp.float32)
        row_term = rowsum_local[:, None] * unit_float - neighbour.reshape(NODE_DEV, D_OUT)
        column_sum = lax.optimization_barrier(jnp.sum(weight_set, axis=2))
        column_term = column_sum[:, :, :, None] * sources - jnp.einsum('rtab,rad->rtbd', weight_set, unit_float.reshape(BLOCKS_DEV, BLOCK, D_OUT), precision=lax.Precision.HIGHEST)
        collected = jnp.zeros((BLOCKS_DEV + RECV_BLOCKS, BLOCK, D_OUT), jnp.float32)
        collected = collected.at[flat_columns].add(column_term.reshape(BLOCKS_DEV * TILES_ROW, BLOCK, D_OUT))
        local_grad = row_term + collected[:BLOCKS_DEV].reshape(NODE_DEV, D_OUT)
        returned = collected[BLOCKS_DEV:].reshape(peer_count, SEND_CAP, D_OUT).astype(jnp.bfloat16)
        return (local_grad, returned)
    local_grad, returned = lax.map(graph_part, (unit_rows, received, weights_dev, columns_dev, rowsum))
    back_values = jnp.swapaxes(returned, 0, 1)

    def collect_back(operands):
        values_local, rows_local, mask_local = operands
        masked = jnp.where(mask_local.reshape(peer_count * SEND_CAP)[:, None], values_local.reshape(peer_count * SEND_CAP, D_OUT).astype(jnp.float32), jnp.zeros((peer_count * SEND_CAP, D_OUT), jnp.float32))
        return jnp.zeros((NODE_DEV, D_OUT), jnp.float32).at[rows_local.reshape(peer_count * SEND_CAP)].add(masked)
    back_sum = lax.map(collect_back, (back_values, send_rows, slot_mask))
    grad_proj = (local_grad + back_sum) * scaling[:, :, None]
    targets = prototypes.astype(jnp.float32)[label_class].reshape(peer_count, LABELS_DEV, D_OUT)
    labels_dev = label_rows.reshape(peer_count, LABELS_DEV)

    def add_labels(operands):
        grad_local, proj_local, rows_local, target_local = operands
        return grad_local.at[rows_local].add(proj_local[rows_local] - target_local)
    grad_proj = lax.map(add_labels, (grad_proj, projected, labels_dev, targets))
    grad_node = grad_proj.astype(jnp.bfloat16)

    def backward(running, operands):
        block_in, grad_local = operands
        pre_act = jnp.dot(block_in, weight_in, preferred_element_type=jnp.float32)
        hidden = gelu_value(pre_act).astype(jnp.bfloat16)
        grad_hidden = jnp.dot(grad_local, weight_out.T, preferred_element_type=jnp.float32)
        grad_pre = (grad_hidden * gelu_slope(pre_act)).astype(jnp.bfloat16)
        embed_local = jnp.dot(grad_pre, weight_in.T, preferred_element_type=jnp.float32).astype(jnp.bfloat16)
        running = running + jnp.dot(hidden.T, grad_local, preferred_element_type=jnp.float32)
        return (running, embed_local)
    running, embed_grad = lax.scan(backward, jnp.zeros((FF, D_OUT), jnp.float32), (inputs_dev, grad_node))
    return (embed_grad.reshape(NODES, D_IN), running * (1.0 / math.sqrt(NODES)))
```

```python
import functools
import math

import jax
import jax.numpy as jnp
from jax import lax
from jax.experimental import pallas as pl
from jax.experimental.pallas import tpu as pltpu
from jax.sharding import PartitionSpec as P

gelu_inner = 0.7978845608028654
gelu_cubic = 0.044715


def gelu_value(values):
    inner_arg = gelu_inner * (values + gelu_cubic * values * values * values)
    return 0.5 * values * (1.0 + jnp.tanh(inner_arg))


def gelu_slope(values):
    inner_arg = gelu_inner * (values + gelu_cubic * values * values * values)
    tangent = jnp.tanh(inner_arg)
    return 0.5 * (1.0 + tangent) + 0.5 * values * (1.0 - tangent * tangent) * gelu_inner * (
        1.0 + 3.0 * gelu_cubic * values * values
    )


MESH = pl.DeviceIdType.MESH
COLOURS = (
    ((0, 1, 2), slice(0, 16), slice(0, 384)),
    ((1, 2, 0), slice(16, 32), slice(0, 384)),
    ((2, 0, 1), slice(0, 32), slice(384, 512)),
)
STRIDES = (16, 4, 1)


def place():
    dom = lax.axis_index("dom")
    return (dom // 16, lax.rem(dom // 4, 4), lax.rem(dom, 4)), lax.axis_index("rep")


def moved(coords, axis, step):
    there = [lax.rem(c + step, 4) if a == axis else c for a, c in enumerate(coords)]
    return there[0] * 16 + there[1] * 4 + there[2]


def enter(coords, core):
    barrier = pltpu.get_barrier_semaphore()
    here = coords[0] * 16 + coords[1] * 4 + coords[2]
    pl.semaphore_signal(barrier, inc=1, device_id=(here, 1 - core), device_id_type=MESH)
    for axis in range(3):
        for step in (1, 2, 3):
            pl.semaphore_signal(
                barrier, inc=1, device_id=(moved(coords, axis, step), core), device_id_type=MESH
            )
    return barrier


def scatter_sum_kernel(
    factor, part_ref, out_ref, mate, b0, b1, b2, r10, r11, r12, s10, s11, s12,
    r20, r21, r22, s20, s21, s22, r30, r31, r32, mate_send, mate_recv, send_sem, recv_sem
):
    coords, core = place()
    here = coords[0] * 16 + coords[1] * 4 + coords[2]
    barrier = enter(coords, core)
    pl.semaphore_wait(barrier, 10)
    swap = pltpu.make_async_remote_copy(
        src_ref=part_ref.at[:, 1 - core],
        dst_ref=mate,
        send_sem=mate_send,
        recv_sem=mate_recv,
        device_id=(here, 1 - core),
        device_id_type=MESH,
    )
    swap.start()
    swap.wait()
    first = (b0, b1, b2)

    def join(chip, carry):
        z, x, y = chip // 16, lax.rem(chip // 4, 4), lax.rem(chip, 4)
        at = (z, x, y)
        total = (
            part_ref[chip, core].astype(jnp.float32) + mate[chip].astype(jnp.float32)
        ).astype(jnp.bfloat16)
        for buffer, (order, rows, cols) in zip(first, COLOURS):
            spot = at[order[0]] * 16 + at[order[1]] * 4 + at[order[2]]
            buffer[spot] = total[rows, cols]
        return carry

    lax.fori_loop(0, 64, join, 0)
    held = [first, (s10, s11, s12), (s20, s21, s22)]
    landing = [(r10, r11, r12), (r20, r21, r22), (r30, r31, r32)]

    def launch(stage, colour):
        axis = COLOURS[colour][0][stage]
        size = STRIDES[stage]
        copies = []
        for step in (1, 2, 3):
            peer = lax.rem(coords[axis] + step, 4)
            copies.append(
                pltpu.make_async_remote_copy(
                    src_ref=held[stage][colour].at[pl.ds(peer * size, size)],
                    dst_ref=landing[stage][colour].at[step - 1],
                    send_sem=send_sem.at[stage, colour, step - 1],
                    recv_sem=recv_sem.at[stage, colour, step - 1],
                    device_id=(moved(coords, axis, step), core),
                    device_id_type=MESH,
                )
            )
        for copy in copies:
            copy.start()
        return copies

    def add(stage, colour, spot):
        axis = COLOURS[colour][0][stage]
        mine = coords[axis] * STRIDES[stage] + spot
        total = held[stage][colour][mine].astype(jnp.float32)
        for step in range(3):
            total = total + landing[stage][colour][step, spot].astype(jnp.float32)
        return total

    flying = [launch(0, colour) for colour in range(3)]
    for stage in range(3):
        after = []
        for colour in range(3):
            for copy in flying[colour]:
                copy.wait()
            if stage < 2:

                def fold(spot, carry, stage=stage, colour=colour):
                    held[stage + 1][colour][spot] = add(stage, colour, spot).astype(jnp.bfloat16)
                    return carry

                lax.fori_loop(0, STRIDES[stage], fold, 0)
                after.append(launch(stage + 1, colour))
            else:
                _, rows, cols = COLOURS[colour]
                out_ref[rows, cols] = add(stage, colour, 0) * factor
        flying = after


def scatter_sum(partial, factor):
    shapes = [(c[1].stop - c[1].start, c[2].stop - c[2].start) for c in COLOURS]
    vmem = lambda *lead: [pltpu.VMEM(lead + s, jnp.bfloat16) for s in shapes]
    return pl.pallas_call(
        functools.partial(scatter_sum_kernel, factor),
        out_shape=jax.ShapeDtypeStruct((32, 512), jnp.float32),
        in_specs=[pl.BlockSpec(memory_space=pltpu.VMEM)],
        out_specs=pl.BlockSpec(memory_space=pltpu.VMEM),
        scratch_shapes=[pltpu.VMEM((64, 32, 512), jnp.bfloat16)]
        + vmem(64)
        + vmem(3, 16)
        + vmem(16)
        + vmem(3, 4)
        + vmem(4)
        + vmem(3, 1)
        + [
            pltpu.SemaphoreType.DMA,
            pltpu.SemaphoreType.DMA,
            pltpu.SemaphoreType.DMA((3, 3, 3)),
            pltpu.SemaphoreType.DMA((3, 3, 3)),
        ],
        compiler_params=pltpu.CompilerParams(
            collective_id=0, has_side_effects=True, vmem_limit_bytes=48 << 20
        ),
        name="scatter_sum",
    )(partial)


def body(
    embeds,
    weight_in,
    weight_out,
    prototypes,
    tile_column,
    tile_weight,
    send_rows,
    send_count,
    label_rows,
    label_class,
):
    node_count = embeds.shape[0]
    block_count = tile_weight.shape[0]
    tile_count = tile_weight.shape[1]
    block_size = tile_weight.shape[2]
    width_out = weight_out.shape[1]
    dom_count = lax.axis_size("dom")
    rep_count = lax.axis_size("rep")
    peer_count = dom_count * rep_count
    slot_count = send_rows.shape[2]
    pre_act = jnp.dot(embeds, weight_in, preferred_element_type=jnp.float32)
    hidden = gelu_value(pre_act).astype(jnp.bfloat16)
    projected = jnp.dot(hidden, weight_out, preferred_element_type=jnp.float32)
    rowsum = jnp.sum(tile_weight, axis=(1, 3), dtype=jnp.float32).reshape(node_count)
    scaling = lax.rsqrt(1.0 + rowsum)
    unit_rows = (projected * scaling[:, None]).astype(jnp.bfloat16)
    slot_mask = (
        lax.broadcasted_iota(jnp.int32, (peer_count, slot_count), 1) < send_count[0][:, None]
    )
    flat_sends = send_rows[0].reshape(peer_count * slot_count)
    outgoing = jnp.take(unit_rows, flat_sends, axis=0).reshape(peer_count, slot_count, width_out)
    outgoing = jnp.where(slot_mask[:, :, None], outgoing, jnp.zeros_like(outgoing))
    incoming = lax.all_to_all(outgoing, ("dom", "rep"), split_axis=0, concat_axis=0, tiled=True)
    incoming = incoming.reshape(peer_count * slot_count, width_out)
    extended = jnp.concatenate([unit_rows, incoming], axis=0).reshape(-1, block_size, width_out)
    total_blocks = extended.shape[0]
    flat_columns = tile_column.reshape(block_count * tile_count)
    sources = jnp.take(extended, flat_columns, axis=0).reshape(
        block_count, tile_count, block_size, width_out
    )
    neighbour = jnp.einsum(
        "rtab,rtbd->rad", tile_weight, sources, preferred_element_type=jnp.float32
    )
    row_term = rowsum[:, None] * unit_rows.astype(jnp.float32) - neighbour.reshape(
        node_count, width_out
    )
    unit_blocks = unit_rows.reshape(block_count, block_size, width_out)
    column_sum = jnp.sum(tile_weight, axis=2, dtype=jnp.float32)
    column_term = column_sum[:, :, :, None] * sources.astype(jnp.float32) - jnp.einsum(
        "rtab,rad->rtbd", tile_weight, unit_blocks, preferred_element_type=jnp.float32
    )
    selector = (
        flat_columns[:, None]
        == lax.broadcasted_iota(jnp.int32, (block_count * tile_count, total_blocks), 1)
    ).astype(jnp.float32)
    gathered_terms = jnp.einsum(
        "tc,tf->cf",
        selector,
        column_term.reshape(block_count * tile_count, block_size * width_out),
        precision=lax.Precision.HIGHEST,
    )
    own_term = gathered_terms[:block_count].reshape(node_count, width_out)
    returned = (
        gathered_terms[block_count:].reshape(peer_count, slot_count, width_out).astype(jnp.bfloat16)
    )
    arrived = lax.all_to_all(returned, ("dom", "rep"), split_axis=0, concat_axis=0, tiled=True)
    back_rows = arrived.reshape(peer_count * slot_count, width_out)
    placement = (
        flat_sends[None, :]
        == lax.broadcasted_iota(jnp.int32, (node_count, peer_count * slot_count), 0)
    ) & slot_mask.reshape(peer_count * slot_count)[None, :]
    back_sum = jnp.dot(
        placement.astype(jnp.bfloat16), back_rows, preferred_element_type=jnp.float32
    )
    grad_proj = (row_term + own_term + back_sum) * scaling[:, None]
    class_table = (
        label_class[:, None]
        == lax.broadcasted_iota(jnp.int32, (label_class.shape[0], prototypes.shape[0]), 1)
    ).astype(jnp.bfloat16)
    targets = jnp.dot(class_table, prototypes, preferred_element_type=jnp.float32)
    grad_proj = grad_proj.at[label_rows].add(jnp.take(projected, label_rows, axis=0) - targets)
    grad_node = grad_proj.astype(jnp.bfloat16)
    grad_hidden = lax.dot_general(
        grad_node, weight_out, (((1,), (1,)), ((), ())), preferred_element_type=jnp.float32
    )
    grad_pre = (grad_hidden * gelu_slope(pre_act)).astype(jnp.bfloat16)
    embed_grad = lax.dot_general(
        grad_pre, weight_in, (((1,), (1,)), ((), ())), preferred_element_type=jnp.float32
    ).astype(jnp.bfloat16)
    factor = 1.0 / math.sqrt(node_count * peer_count)
    partial = lax.dot_general(
        hidden, grad_node, (((0,), (0,)), ((), ())), preferred_element_type=jnp.float32
    ).astype(jnp.bfloat16)
    grad_weight = scatter_sum(partial.reshape(peer_count // 2, 2, -1, width_out), factor)
    return (embed_grad, grad_weight)


def solution(mesh):
    placed = (
        P(("dom", "rep"), None),
        P(),
        P(),
        P(),
        P(("dom", "rep"), None),
        P(("dom", "rep"), None, None, None),
        P(("dom", "rep"), None, None),
        P(("dom", "rep"), None),
        P(("dom", "rep")),
        P(("dom", "rep")),
    )
    return jax.shard_map(
        body,
        mesh=mesh,
        in_specs=placed,
        out_specs=(P(("dom", "rep"), None), P(("dom", "rep"), None)),
        check_vma=False,
    )
```

```python
import functools
import math

import jax
import jax.numpy as jnp
from jax import lax
from jax.experimental import pallas as pl
from jax.experimental.pallas import tpu as pltpu
from jax.sharding import PartitionSpec as P

gelu_inner = 0.7978845608028654
gelu_cubic = 0.044715


def gelu_value(values):
    inner_arg = gelu_inner * (values + gelu_cubic * values * values * values)
    return 0.5 * values * (1.0 + jnp.tanh(inner_arg))


def gelu_slope(values):
    inner_arg = gelu_inner * (values + gelu_cubic * values * values * values)
    tangent = jnp.tanh(inner_arg)
    return 0.5 * (1.0 + tangent) + 0.5 * values * (1.0 - tangent * tangent) * gelu_inner * (
        1.0 + 3.0 * gelu_cubic * values * values
    )


MESH = pl.DeviceIdType.MESH
COLOURS = (
    ((0, 1, 2), slice(0, 16), slice(0, 384)),
    ((1, 2, 0), slice(16, 32), slice(0, 384)),
    ((2, 0, 1), slice(0, 32), slice(384, 512)),
)
STRIDES = (16, 4, 1)


def place():
    dom = lax.axis_index("dom")
    return (dom // 16, lax.rem(dom // 4, 4), lax.rem(dom, 4)), lax.axis_index("rep")


def moved(coords, axis, step):
    there = [lax.rem(c + step, 4) if a == axis else c for a, c in enumerate(coords)]
    return there[0] * 16 + there[1] * 4 + there[2]


def enter(coords, core):
    barrier = pltpu.get_barrier_semaphore()
    here = coords[0] * 16 + coords[1] * 4 + coords[2]
    pl.semaphore_signal(barrier, inc=1, device_id=(here, 1 - core), device_id_type=MESH)
    for axis in range(3):
        for step in (1, 2, 3):
            pl.semaphore_signal(
                barrier, inc=1, device_id=(moved(coords, axis, step), core), device_id_type=MESH
            )
    return barrier


def scatter_sum_kernel(
    factor, part_ref, out_ref, mate, b0, b1, b2, r10, r11, r12, s10, s11, s12,
    r20, r21, r22, s20, s21, s22, r30, r31, r32, mate_send, mate_recv, send_sem, recv_sem
):
    coords, core = place()
    here = coords[0] * 16 + coords[1] * 4 + coords[2]
    barrier = enter(coords, core)
    pl.semaphore_wait(barrier, 10)
    swap = pltpu.make_async_remote_copy(
        src_ref=part_ref.at[:, 1 - core],
        dst_ref=mate,
        send_sem=mate_send,
        recv_sem=mate_recv,
        device_id=(here, 1 - core),
        device_id_type=MESH,
    )
    swap.start()
    swap.wait()
    first = (b0, b1, b2)

    def join(chip, carry):
        z, x, y = chip // 16, lax.rem(chip // 4, 4), lax.rem(chip, 4)
        at = (z, x, y)
        total = (
            part_ref[chip, core].astype(jnp.float32) + mate[chip].astype(jnp.float32)
        ).astype(jnp.bfloat16)
        for buffer, (order, rows, cols) in zip(first, COLOURS):
            spot = at[order[0]] * 16 + at[order[1]] * 4 + at[order[2]]
            buffer[spot] = total[rows, cols]
        return carry

    lax.fori_loop(0, 64, join, 0)
    held = [first, (s10, s11, s12), (s20, s21, s22)]
    landing = [(r10, r11, r12), (r20, r21, r22), (r30, r31, r32)]

    def launch(stage, colour):
        axis = COLOURS[colour][0][stage]
        size = STRIDES[stage]
        copies = []
        for step in (1, 2, 3):
            peer = lax.rem(coords[axis] + step, 4)
            copies.append(
                pltpu.make_async_remote_copy(
                    src_ref=held[stage][colour].at[pl.ds(peer * size, size)],
                    dst_ref=landing[stage][colour].at[step - 1],
                    send_sem=send_sem.at[stage, colour, step - 1],
                    recv_sem=recv_sem.at[stage, colour, step - 1],
                    device_id=(moved(coords, axis, step), core),
                    device_id_type=MESH,
                )
            )
        for copy in copies:
            copy.start()
        return copies

    def add(stage, colour, spot):
        axis = COLOURS[colour][0][stage]
        mine = coords[axis] * STRIDES[stage] + spot
        total = held[stage][colour][mine].astype(jnp.float32)
        for step in range(3):
            total = total + landing[stage][colour][step, spot].astype(jnp.float32)
        return total

    flying = [launch(0, colour) for colour in range(3)]
    for stage in range(3):
        after = []
        for colour in range(3):
            for copy in flying[colour]:
                copy.wait()
            if stage < 2:

                def fold(spot, carry, stage=stage, colour=colour):
                    held[stage + 1][colour][spot] = add(stage, colour, spot).astype(jnp.bfloat16)
                    return carry

                lax.fori_loop(0, STRIDES[stage], fold, 0)
                after.append(launch(stage + 1, colour))
            else:
                _, rows, cols = COLOURS[colour]
                out_ref[rows, cols] = add(stage, colour, 0) * factor
        flying = after


def scatter_sum(partial, factor):
    shapes = [(c[1].stop - c[1].start, c[2].stop - c[2].start) for c in COLOURS]
    vmem = lambda *lead: [pltpu.VMEM(lead + s, jnp.bfloat16) for s in shapes]
    return pl.pallas_call(
        functools.partial(scatter_sum_kernel, factor),
        out_shape=jax.ShapeDtypeStruct((32, 512), jnp.float32),
        in_specs=[pl.BlockSpec(memory_space=pltpu.VMEM)],
        out_specs=pl.BlockSpec(memory_space=pltpu.VMEM),
        scratch_shapes=[pltpu.VMEM((64, 32, 512), jnp.bfloat16)]
        + vmem(64)
        + vmem(3, 16)
        + vmem(16)
        + vmem(3, 4)
        + vmem(4)
        + vmem(3, 1)
        + [
            pltpu.SemaphoreType.DMA,
            pltpu.SemaphoreType.DMA,
            pltpu.SemaphoreType.DMA((3, 3, 3)),
            pltpu.SemaphoreType.DMA((3, 3, 3)),
        ],
        compiler_params=pltpu.CompilerParams(
            collective_id=0, has_side_effects=True, vmem_limit_bytes=48 << 20
        ),
        name="scatter_sum",
    )(partial)


BLOCK = 128
FIRST = (((0,), (0,)), ((), ()))


def block_rows(index):
    return pl.ds(pl.multiple_of(index * BLOCK, BLOCK), BLOCK)


def pieces_of(sums):
    high = sums.astype(jnp.bfloat16)
    rest = sums - high.astype(jnp.float32)
    middle = rest.astype(jnp.bfloat16)
    low = (rest - middle.astype(jnp.float32)).astype(jnp.bfloat16)
    lane = lax.broadcasted_iota(jnp.int32, sums.shape, 1)
    wide = [piece.astype(jnp.float32) for piece in (high, middle, low)]
    chosen = jnp.where(lane == 0, wide[0], jnp.where(lane == 1, wide[1], wide[2]))
    return jnp.where(lane < 3, chosen, 0.0).astype(jnp.bfloat16)


def outgoing_kernel(column_ref, projected_ref, weight_ref, sends_ref, unit_ref, rowsum_ref, out_ref, total):
    width = projected_ref.shape[1]
    ones = jnp.ones((BLOCK, BLOCK), jnp.bfloat16)
    for block in range(4):
        rows = slice(block * BLOCK, (block + 1) * BLOCK)
        joined = weight_ref[block * 8].astype(jnp.float32)
        for tile in range(1, 8):
            joined = joined + weight_ref[block * 8 + tile].astype(jnp.float32)
        rowsum = jnp.sum(joined, axis=1, keepdims=True)
        rowsum_ref[rows] = jnp.broadcast_to(rowsum, (BLOCK, BLOCK))
        unit_ref[rows] = (projected_ref[rows] * lax.rsqrt(1.0 + rowsum)).astype(jnp.bfloat16)
    total[...] = jnp.zeros_like(total)
    for block in range(4):
        rows = slice(block * BLOCK, (block + 1) * BLOCK)
        operand = jnp.concatenate([unit_ref[rows], ones], axis=1)
        for tile in range(4, 8):
            spot = column_ref[block, tile] - 4
            total[spot] += lax.dot_general(
                weight_ref[block * 8 + tile], operand, FIRST, preferred_element_type=jnp.float32
            )
    unit = unit_ref[...]
    for block in range(8):
        rows = slice(block * BLOCK, (block + 1) * BLOCK)
        picks = (
            sends_ref[rows] == lax.broadcasted_iota(jnp.int32, (BLOCK, unit.shape[0]), 1)
        ).astype(jnp.bfloat16)
        out_ref[rows, :width] = jnp.dot(picks, unit, preferred_element_type=jnp.float32).astype(
            jnp.bfloat16
        )
        out_ref[rows, width : 2 * width] = total[block, :, :width].astype(jnp.bfloat16)
        out_ref[rows, 2 * width :] = pieces_of(total[block, :, width:])


def local_kernel(
    column_ref, projected_ref, unit_ref, rowsum_ref, weight_ref, label_rows_ref, label_class_ref,
    prototypes_ref, base_ref, total
):
    width = projected_ref.shape[1]
    ones = jnp.ones((BLOCK, BLOCK), jnp.bfloat16)
    total[...] = jnp.zeros_like(total)
    classes = prototypes_ref.shape[0]
    labels = label_rows_ref.shape[1]
    table = (
        label_class_ref[...] == lax.broadcasted_iota(jnp.int32, (labels, classes), 1)
    ).astype(jnp.bfloat16)
    targets = jnp.dot(table, prototypes_ref[...], preferred_element_type=jnp.float32).astype(
        jnp.bfloat16
    )
    for block in range(4):
        rows = slice(block * BLOCK, (block + 1) * BLOCK)
        operand = jnp.concatenate([unit_ref[rows], ones], axis=1)
        near = jnp.zeros((BLOCK, width), jnp.float32)
        for tile in range(4):
            spot = column_ref[block, tile]
            weight = weight_ref[block * 8 + tile]
            total[spot] += lax.dot_general(
                weight, operand, FIRST, preferred_element_type=jnp.float32
            )
            near = near + jnp.dot(
                weight, unit_ref[block_rows(spot)], preferred_element_type=jnp.float32
            )
        base_ref[rows] = near
    for block in range(4):
        rows = slice(block * BLOCK, (block + 1) * BLOCK)
        rowsum = rowsum_ref[rows, :1]
        unit = unit_ref[rows].astype(jnp.float32)
        row_term = rowsum * unit - base_ref[rows]
        own_term = total[block, :, width : width + 1] * unit - total[block, :, :width]
        spots = label_rows_ref[...] == (
            lax.broadcasted_iota(jnp.int32, (BLOCK, labels), 0) + block * BLOCK
        )
        marked = jnp.sum(spots.astype(jnp.float32), axis=1, keepdims=True)
        wanted = jnp.dot(
            spots.astype(jnp.bfloat16), targets, preferred_element_type=jnp.float32
        )
        base_ref[rows] = (row_term + own_term) * lax.rsqrt(1.0 + rowsum) + (
            marked * projected_ref[rows] - wanted
        )


def merge_kernel(
    column_ref, message_ref, unit_ref, rowsum_ref, base_ref, weight_ref, sends_ref, grad_ref
):
    width = unit_ref.shape[1]
    slots = message_ref.shape[0]
    for block in range(4):
        rows = slice(block * BLOCK, (block + 1) * BLOCK)
        picks = (
            sends_ref[...]
            == lax.broadcasted_iota(jnp.int32, (BLOCK, slots), 0) + block * BLOCK
        ).astype(jnp.bfloat16)
        back = jnp.dot(picks, message_ref[:, width:], preferred_element_type=jnp.float32)
        sums = back[:, width : width + 1] + back[:, width + 1 : width + 2]
        sums = sums + back[:, width + 2 : width + 3]
        far = sums * unit_ref[rows].astype(jnp.float32) - back[:, :width]
        for tile in range(4, 8):
            spot = column_ref[block, tile] - 4
            far = far - jnp.dot(
                weight_ref[block * 8 + tile],
                message_ref[block_rows(spot), :width],
                preferred_element_type=jnp.float32,
            )
        grad_ref[rows] = (
            base_ref[rows] + far * lax.rsqrt(1.0 + rowsum_ref[rows, :1])
        ).astype(jnp.bfloat16)


def on_core(kernel, name, count, outs, scratch=(), flops=0, moved_bytes=0):
    return pl.pallas_call(
        kernel,
        out_shape=outs,
        in_specs=[pl.BlockSpec(memory_space=pltpu.SMEM)]
        + [pl.BlockSpec(memory_space=pltpu.VMEM)] * (count - 1),
        out_specs=jax.tree.map(lambda _: pl.BlockSpec(memory_space=pltpu.VMEM), outs),
        scratch_shapes=list(scratch),
        cost_estimate=pl.CostEstimate(
            flops=flops, bytes_accessed=moved_bytes, transcendentals=0
        ),
        compiler_params=pltpu.CompilerParams(vmem_limit_bytes=48 << 20),
        name=name,
    )


def body(
    embeds,
    weight_in,
    weight_out,
    prototypes,
    tile_column,
    tile_weight,
    send_rows,
    send_count,
    label_rows,
    label_class,
):
    node_count = embeds.shape[0]
    width_out = weight_out.shape[1]
    dom_count = lax.axis_size("dom")
    rep_count = lax.axis_size("rep")
    peer_count = dom_count * rep_count
    slot_count = send_rows.shape[2]
    slots = peer_count * slot_count
    message = 2 * width_out + BLOCK
    slot_mask = (
        lax.broadcasted_iota(jnp.int32, (peer_count, slot_count), 1) < send_count[0][:, None]
    )
    sends = jnp.where(slot_mask, send_rows[0], -1)
    pre_act = jnp.dot(embeds, weight_in, preferred_element_type=jnp.float32)
    hidden = gelu_value(pre_act).astype(jnp.bfloat16)
    projected = jnp.dot(hidden, weight_out, preferred_element_type=jnp.float32)
    weights = tile_weight.reshape(-1, BLOCK, BLOCK)
    unit_rows, rowsum, outgoing = on_core(
        outgoing_kernel,
        "outgoing",
        4,
        (
            jax.ShapeDtypeStruct((node_count, width_out), jnp.bfloat16),
            jax.ShapeDtypeStruct((node_count, BLOCK), jnp.float32),
            jax.ShapeDtypeStruct((slots, message), jnp.bfloat16),
        ),
        [pltpu.VMEM((8, BLOCK, width_out + BLOCK), jnp.float32)],
    )(tile_column, projected, weights, sends.reshape(slots, 1))
    arrived = lax.all_to_all(
        outgoing.reshape(peer_count, slot_count, message),
        ("dom", "rep"),
        split_axis=0,
        concat_axis=0,
        tiled=True,
    ).reshape(slots, message)
    base = on_core(
        local_kernel,
        "local_terms",
        8,
        jax.ShapeDtypeStruct((node_count, width_out), jnp.float32),
        [pltpu.VMEM((4, BLOCK, width_out + BLOCK), jnp.float32)],
        flops=2 * 32 * 128 * 128 * 640,
        moved_bytes=6 << 20,
    )(
        tile_column,
        projected,
        unit_rows,
        rowsum,
        weights,
        label_rows.reshape(1, -1),
        label_class.reshape(-1, 1),
        prototypes,
    )
    grad_node = on_core(
        merge_kernel,
        "merge",
        7,
        jax.ShapeDtypeStruct((node_count, width_out), jnp.bfloat16),
    )(tile_column, arrived, unit_rows, rowsum, base, weights, sends.reshape(1, slots))
    grad_hidden = lax.dot_general(
        grad_node, weight_out, (((1,), (1,)), ((), ())), preferred_element_type=jnp.float32
    )
    grad_pre = (grad_hidden * gelu_slope(pre_act)).astype(jnp.bfloat16)
    embed_grad = lax.dot_general(
        grad_pre, weight_in, (((1,), (1,)), ((), ())), preferred_element_type=jnp.float32
    ).astype(jnp.bfloat16)
    factor = 1.0 / math.sqrt(node_count * peer_count)
    partial = lax.dot_general(
        hidden, grad_node, (((0,), (0,)), ((), ())), preferred_element_type=jnp.float32
    ).astype(jnp.bfloat16)
    grad_weight = scatter_sum(partial.reshape(peer_count // 2, 2, -1, width_out), factor)
    return (embed_grad, grad_weight)


def solution(mesh):
    placed = (
        P(("dom", "rep"), None),
        P(),
        P(),
        P(),
        P(("dom", "rep"), None),
        P(("dom", "rep"), None, None, None),
        P(("dom", "rep"), None, None),
        P(("dom", "rep"), None),
        P(("dom", "rep")),
        P(("dom", "rep")),
    )
    return jax.shard_map(
        body,
        mesh=mesh,
        in_specs=placed,
        out_specs=(P(("dom", "rep"), None), P(("dom", "rep"), None)),
        check_vma=False,
    )
```
